256 devices in a mesh: dp: 4 (over z_hi), row: 16 (over y, x), col: 4 (over z_lo, core).
Axes of the slice: x: 4, y: 4, z: 8 (z_hi: 4, z_lo: 2; z = z_hi * 2 + z_lo), core: 2. Of those that a mesh axis runs over, the one named last changes fastest.
Arguments:
- grad_partials: float32 [4, 4, 2048, 16384], P('dp', None, 'row', 'col'), may hold values from -300 to 300, as said below
- master_weights: float32 [8192, 16384], P(('dp', 'row'), 'col'), may hold values from -1.5 to 1.5
- row_moment: float32 [8192], P(('dp', 'row')), may hold values from 0.3 to 30
- col_moment: float32 [16384], P('col'), may hold values from 0.003 to 0.3
Outputs:
- new_master: float32 [8192, 16384], P(('dp', 'row'), 'col')
- new_row_moment: float32 [8192], P(('dp', 'row'))
- new_col_moment: float32 [16384], P('col')
- compute_weights: bfloat16 [4, 2048, 16384], P(None, 'row', 'col')
- rms_update: float32 [], replicated
The draws below stay inside these ranges and needn't reach their ends.
Inputs may be any that keep to these rules, and one draw needn't show every extreme that they name: `grad_partials`: finite gradient partials.
All inputs are finite; a program needn't handle non-finite values.
Results may differ from the reference program's by a relative error of at most 0.0004.
Values may be sent and summed in bfloat16 or wider, within the bound.
A program may use at most 128 MiB of HBM per device.

```python
import math
import jax
import jax.numpy as jnp
from jax import lax

D = 16384
ROWS = 8192
N_DP = 4


def draw_grad_partials(key, part):
    quarter = ROWS // N_DP
    key_row, key_col, key_own = jax.random.split(key, 3)
    row_index = jnp.arange(ROWS, dtype=jnp.float32)
    col_index = jnp.arange(D, dtype=jnp.float32)
    row_scale = jnp.exp(jax.random.uniform(key_row, (ROWS,), jnp.float32, math.log(0.3), math.log(3.0))) * jnp.exp(math.log(30.0) * (row_index / ROWS - 1.0))
    col_scale = jnp.exp(jax.random.uniform(key_col, (D,), jnp.float32, math.log(0.3), math.log(3.0))) * (0.6 + 1.2 * col_index / D)
    shape = (N_DP, N_DP, quarter, D)
    noise = 3.0 * jax.random.truncated_normal(key_own, -4.0, 4.0, shape, jnp.float32)
    scales = row_scale.reshape(1, N_DP, quarter, 1) * col_scale.reshape(1, 1, 1, D)
    return noise * scales


def steps_of(rng, extent, shards, low, largest):
    gain, own = 1.0, jax.random.fold_in(rng, 6)
    for axis_at, blocks in shards:
        heights = jnp.exp(jax.random.uniform(jax.random.fold_in(own, axis_at), (blocks,), jnp.float32, low / len(shards), largest / len(shards)))
        gain = gain * jnp.repeat(heights, extent[axis_at] // blocks).reshape([-1 if axis == axis_at else 1 for axis in range(len(extent))])
    return gain


def setup_inputs(seed: int = 0) -> dict:
    splits = jax.random.split(jax.random.key(seed), 5)
    return {
        "grad_partials": draw_grad_partials(jax.random.fold_in(splits[4], 71), 0),
        "master_weights": jnp.clip(jax.random.uniform(splits[1], (ROWS, D), jnp.float32, -1.5, 1.5) * steps_of(splits[1], (ROWS, D), ((0, 64), (1, 4)), -0.4, 0.0), -1.5, 1.5),
        "row_moment": jnp.clip(jnp.exp(math.log(30.0) - 4.6051701 * jax.random.uniform(splits[2], (ROWS,), jnp.float32) ** steps_of(splits[2], (ROWS,), ((0, 64),), -0.2, 0.2)), 0.3, 30.0),
        "col_moment": jnp.clip(jnp.exp(math.log(0.3) - 4.6051702 * jax.random.uniform(splits[3], (D,), jnp.float32) ** steps_of(splits[3], (D,), ((0, 4),), -0.2, 0.2)), 0.003, 0.3),
    }


decay_rate = 0.9
step_rate = 0.05
tiny_value = 1e-30

def reference(grad_partials, master_weights, row_moment, col_moment):
    gradient = lax.optimization_barrier(jnp.sum(grad_partials, axis=0)).reshape(ROWS, D)
    squared = gradient * gradient
    row_mean = lax.optimization_barrier(jnp.sum(squared, axis=1)) / D + tiny_value
    col_mean = lax.optimization_barrier(jnp.sum(squared, axis=0)) / ROWS + tiny_value
    new_rows = decay_rate * row_moment + (1.0 - decay_rate) * row_mean
    new_cols = decay_rate * col_moment + (1.0 - decay_rate) * col_mean
    scale_mean = jnp.mean(new_rows)
    update = gradient * lax.rsqrt(new_rows[:, None] * new_cols[None, :] / scale_mean)
    rms_update = jnp.sqrt(jnp.mean(update * update))
    new_weights = master_weights - step_rate * update / jnp.maximum(1.0, rms_update)
    copies = new_weights.astype(jnp.bfloat16).reshape(N_DP, ROWS // N_DP, D)
    return (new_weights, new_rows, new_cols, copies, rms_update)
```

```python
import functools

import jax
import jax.numpy as jnp
from jax import lax
from jax.experimental import pallas as pl
from jax.experimental.pallas import tpu as pltpu
from jax.sharding import PartitionSpec as P

decay_rate = 0.9
step_rate = 0.05
tiny_value = 1e-30

MESH = pl.DeviceIdType.MESH
LANES = 128
X_SIZE = 4
RS_ROWS = 8
AG_ROWS = 16


def kernel(all_rows, full_width, grads, master, row_mom, col_mom,
           new_master, new_rows, new_cols, copies, rms_out,
           opp_l, opp_r, add_r, add_l, own_l, own_r, mine, mast, wb,
           row_part, col_part, inv_cols, inv_rows, x_buf, y_buf, d_buf, r_buf,
           s_bufs, load_sem, rs_send, rs_recv, st_send, st_recv, ag_send, ag_recv, out_sem):
    dp, row, col = lax.axis_index("dp"), lax.axis_index("row"), lax.axis_index("col")
    y, x = row // X_SIZE, row % X_SIZE
    right, left, far = (dp + 1) % 4, (dp + 3) % 4, (dp + 2) % 4
    rows, width = mine.shape
    half = rows // 2
    rs_n = half // RS_ROWS
    groups = width // LANES

    def x_peer(j):
        return {"row": y * X_SIZE + (x + j) % X_SIZE}

    def y_peer(j):
        return {"row": ((y + j) % 4) * X_SIZE + x}

    def d_peer(j):
        return {"dp": (dp + j) % 4}

    def c_peer(j):
        return {"col": (col + j) % 4}

    loads = [
        pltpu.make_async_copy(grads.at[0, right, pl.ds(0, half)], add_r, load_sem.at[0]),
        pltpu.make_async_copy(grads.at[0, left, pl.ds(half, half)], add_l, load_sem.at[1]),
        pltpu.make_async_copy(grads.at[0, dp], mine, load_sem.at[2]),
        pltpu.make_async_copy(master, mast, load_sem.at[3]),
    ]
    for load in loads:
        load.start()

    barrier = pltpu.get_barrier_semaphore()
    for peer in (x_peer, y_peer, d_peer, c_peer):
        for j in (1, 2, 3):
            pl.semaphore_signal(barrier, inc=1, device_id=peer(j), device_id_type=MESH)
    pl.semaphore_wait(barrier, 12)

    def rs_copy(way, phase, k):
        to = right if way == 0 else left
        at = pl.multiple_of(k * RS_ROWS, RS_ROWS)
        low, high = pl.ds(at, RS_ROWS), pl.ds(pl.multiple_of(half + at, RS_ROWS), RS_ROWS)
        near, other = (low, high) if way == 0 else (high, low)
        opp, own, add = (opp_l, own_l, add_r) if way == 0 else (opp_r, own_r, add_l)
        if phase == 0:
            src, dst = grads.at[0, far, near], opp.at[low]
        elif phase == 1:
            src, dst = grads.at[0, to, other], own.at[other]
        else:
            src, dst = add.at[low], own.at[near]
        return pltpu.make_async_remote_copy(
            src_ref=src, dst_ref=dst, send_sem=rs_send.at[way, phase, k], recv_sem=rs_recv.at[way, phase, k],
            device_id={"dp": to}, device_id_type=MESH)

    @pl.loop(0, rs_n)
    def _(k):
        rs_copy(0, 0, k).start()
        rs_copy(1, 0, k).start()

    loads[0].wait()
    loads[1].wait()

    @pl.loop(0, rs_n)
    def _(k):
        at = pl.ds(pl.multiple_of(k * RS_ROWS, RS_ROWS), RS_ROWS)
        rs_copy(0, 1, k).start()
        rs_copy(1, 1, k).start()
        rs_copy(0, 0, k).wait_recv()
        add_r[at] = add_r[at] + opp_l[at]
        rs_copy(0, 2, k).start()
        rs_copy(1, 0, k).wait_recv()
        add_l[at] = add_l[at] + opp_r[at]
        rs_copy(1, 2, k).start()

    loads[2].wait()
    col_part[...] = jnp.zeros_like(col_part)

    def take(at):
        total = jnp.zeros((RS_ROWS, LANES), jnp.float32)
        for c in range(groups):
            lanes = pl.ds(c * LANES, LANES)
            g = mine[at, lanes] + own_l[at, lanes] + own_r[at, lanes]
            mine[at, lanes] = g
            square = g * g
            total = total + square
            col_part[:, lanes] = col_part[:, lanes] + square
        row_part[at] = total

    @pl.loop(0, rs_n)
    def _(k):
        at = k * RS_ROWS
        rs_copy(1, 1, k).wait_recv()
        rs_copy(0, 2, k).wait_recv()
        take(pl.ds(pl.multiple_of(at, RS_ROWS), RS_ROWS))
        rs_copy(0, 1, k).wait_recv()
        rs_copy(1, 2, k).wait_recv()
        take(pl.ds(pl.multiple_of(half + at, RS_ROWS), RS_ROWS))

    def exchange(stage, buf, me, peer):
        def one(j):
            return pltpu.make_async_remote_copy(
                src_ref=buf.at[me], dst_ref=buf.at[me], send_sem=st_send.at[stage, j - 1],
                recv_sem=st_recv.at[stage, j - 1], device_id=peer(j), device_id_type=MESH)
        for j in (1, 2, 3):
            one(j).start()
        return one

    def finish(one):
        for j in (1, 2, 3):
            one(j).wait_recv()

    def total_of(buf):
        return (buf[0] + buf[1]) + (buf[2] + buf[3])

    x_buf[x] = jnp.sum(col_part[...], axis=0, keepdims=True)
    x_copy = exchange(0, x_buf, x, x_peer)
    eye = lax.broadcasted_iota(jnp.int32, (rows, LANES), 0) == lax.broadcasted_iota(jnp.int32, (rows, LANES), 1)
    row_sums = jnp.sum(row_part[...], axis=1, keepdims=True)
    r_buf[col] = jnp.sum(jnp.where(eye, row_sums, 0.0), axis=0, keepdims=True)
    r_copy = exchange(1, r_buf, col, c_peer)
    finish(x_copy)
    y_buf[y] = total_of(x_buf)
    y_copy = exchange(2, y_buf, y, y_peer)
    finish(r_copy)
    row_mean = total_of(r_buf) / full_width + tiny_value
    next_rows = decay_rate * row_mom[...] + (1.0 - decay_rate) * row_mean
    new_rows[...] = next_rows
    rows_down = jnp.sum(jnp.where(eye, next_rows, 0.0), axis=1, keepdims=True)
    inv_rows[...] = jnp.broadcast_to(1.0 / rows_down, inv_rows.shape)
    finish(y_copy)
    d_buf[dp] = total_of(y_buf)
    d_copy = exchange(3, d_buf, dp, d_peer)
    finish(d_copy)
    col_mean = total_of(d_buf) / all_rows + tiny_value
    next_cols = decay_rate * col_mom[...] + (1.0 - decay_rate) * col_mean
    new_cols[...] = next_cols
    inv_cols[...] = jnp.broadcast_to(1.0 / next_cols, inv_cols.shape)

    def add_squares(k, acc):
        at = pl.ds(pl.multiple_of(k * 8, 8), 8)
        part = jnp.zeros((8, LANES), jnp.float32)
        for c in range(groups):
            lanes = pl.ds(c * LANES, LANES)
            g = mine[at, lanes]
            part = part + g * g * inv_cols[:, lanes]
        return acc + part * inv_rows[at]

    squares = lax.fori_loop(0, rows // 8, add_squares, jnp.zeros((8, LANES), jnp.float32))

    first = lax.broadcasted_iota(jnp.int32, (8, LANES), 0) == 0
    s_bufs[0, col, 0] = squares
    s_bufs[0, col, 1] = jnp.where(first, jnp.broadcast_to(next_rows, (8, LANES)), 0.0)
    for stage, (me, peer) in enumerate(((col, c_peer), (x, x_peer), (y, y_peer), (dp, d_peer))):
        finish(exchange(4 + stage, s_bufs.at[stage], me, peer))
        both = total_of(s_bufs.at[stage])
        if stage < 3:
            s_bufs[stage + 1, (x, y, dp)[stage]] = both
    scale_mean = jnp.sum(both[1], axis=(0, 1), keepdims=True) / (4.0 * all_rows)
    update_sum = jnp.sum(both[0], axis=(0, 1), keepdims=True) * scale_mean
    rms_update = jnp.sqrt(update_sum / (float(all_rows) * float(full_width)))
    rms_out[...] = rms_update
    factor = step_rate * jnp.sqrt(scale_mean) / jnp.maximum(1.0, rms_update)
    inv_cols[...] = jnp.sqrt(inv_cols[...]) * factor
    inv_rows[...] = jnp.sqrt(inv_rows[...])
    loads[3].wait()

    ag_n = rows // AG_ROWS

    def ag_copy(way, k, passed):
        to = right if way == 0 else left
        at = pl.ds(pl.multiple_of(k * AG_ROWS, AG_ROWS), AG_ROWS)
        if passed:
            slot = left if way == 0 else right
            src, sem = copies.at[slot, at], ag_n + k % (ag_n // 2)
        else:
            slot, src, sem = dp, wb.at[at], k
        return pltpu.make_async_remote_copy(
            src_ref=src, dst_ref=copies.at[slot, at], send_sem=ag_send.at[way, sem], recv_sem=ag_recv.at[way, sem],
            device_id={"dp": to}, device_id_type=MESH)

    def ag_arrived(way, k, passed):
        return ag_copy(way, k, passed)

    def out_copies(k):
        at = pl.ds(pl.multiple_of(k * AG_ROWS, AG_ROWS), AG_ROWS)
        return (pltpu.make_async_copy(mast.at[at], new_master.at[at], out_sem.at[0, k]),
                pltpu.make_async_copy(wb.at[at], copies.at[dp, at], out_sem.at[1, k]))

    def give(k):
        base = pl.multiple_of(k * AG_ROWS, AG_ROWS)
        at = pl.ds(base, AG_ROWS)
        scale = inv_rows[at]
        for c in range(groups):
            lanes = pl.ds(c * LANES, LANES)
            across = inv_cols[:, lanes]
            across = jnp.concatenate([across, across], axis=0)
            w = mast[at, lanes] - mine[at, lanes] * scale * across
            mast[at, lanes] = w
            wb[at, lanes] = w.astype(jnp.bfloat16)

    ag_half = ag_n // 2

    @pl.loop(0, ag_half)
    def _(k):
        give(k)
        ag_copy(0, k, False).start()
        give(k + ag_half)
        ag_copy(1, k + ag_half, False).start()

    @pl.loop(0, ag_half)
    def _(k):
        ag_copy(0, k + ag_half, False).start()
        ag_copy(1, k, False).start()
        for o in (k, k + ag_half):
            for c in out_copies(o):
                c.start()

    @pl.loop(0, ag_half)
    def _(k):
        ag_copy(0, k, False).wait_recv()
        ag_copy(0, k, True).start()
        ag_copy(1, k + ag_half, False).wait_recv()
        ag_copy(1, k + ag_half, True).start()

    @pl.loop(0, ag_half)
    def _(k):
        ag_copy(0, k + ag_half, False).wait_recv()
        ag_copy(1, k, False).wait_recv()
        ag_copy(0, k, True).wait_recv()
        ag_copy(1, k + ag_half, True).wait_recv()
        ag_copy(0, k, True).wait_send()
        ag_copy(1, k + ag_half, True).wait_send()
        for o in (k, k + ag_half):
            ag_copy(0, o, False).wait_send()
            ag_copy(1, o, False).wait_send()
            for c in out_copies(o):
                c.wait()

    @pl.loop(0, rs_n)
    def _(k):
        for way in (0, 1):
            for phase in (0, 1, 2):
                rs_copy(way, phase, k).wait_send()

    stages = ((x_buf, x, x_peer), (r_buf, col, c_peer), (y_buf, y, y_peer), (d_buf, dp, d_peer),
              (s_bufs.at[0], col, c_peer), (s_bufs.at[1], x, x_peer), (s_bufs.at[2], y, y_peer), (s_bufs.at[3], dp, d_peer))
    for stage, (buf, me, peer) in enumerate(stages):
        for j in (1, 2, 3):
            pltpu.make_async_remote_copy(
                src_ref=buf.at[me], dst_ref=buf.at[me], send_sem=st_send.at[stage, j - 1],
                recv_sem=st_recv.at[stage, j - 1], device_id=peer(j), device_id_type=MESH).wait_send()


def local(grad_partials, master_weights, row_moment, col_moment):
    rows, width = master_weights.shape
    all_rows = rows * lax.axis_size("dp") * lax.axis_size("row")
    full_width = width * lax.axis_size("col")
    half = rows // 2
    rs_n, ag_n = half // RS_ROWS, rows // AG_ROWS
    f32 = jnp.float32
    anywhere = pl.BlockSpec(memory_space=pl.ANY)
    vmem = pl.BlockSpec(memory_space=pltpu.VMEM)
    new_master, new_rows, new_cols, copies, rms = pl.pallas_call(
        functools.partial(kernel, all_rows, full_width),
        out_shape=(
            jax.ShapeDtypeStruct((rows, width), f32),
            jax.ShapeDtypeStruct((1, rows), f32),
            jax.ShapeDtypeStruct((1, width), f32),
            jax.ShapeDtypeStruct((4, rows, width), jnp.bfloat16),
            jax.ShapeDtypeStruct((1, 1), f32),
        ),
        in_specs=[anywhere, anywhere, vmem, vmem],
        out_specs=(anywhere, vmem, vmem, anywhere, vmem),
        scratch_shapes=[
            pltpu.VMEM((half, width), f32), pltpu.VMEM((half, width), f32),
            pltpu.VMEM((half, width), f32), pltpu.VMEM((half, width), f32),
            pltpu.VMEM((rows, width), f32), pltpu.VMEM((rows, width), f32),
            pltpu.VMEM((rows, width), f32), pltpu.VMEM((rows, width), f32),
            pltpu.VMEM((rows, width), jnp.bfloat16),
            pltpu.VMEM((rows, LANES), f32), pltpu.VMEM((8, width), f32), pltpu.VMEM((8, width), f32),
            pltpu.VMEM((rows, LANES), f32),
            pltpu.VMEM((4, 1, width), f32), pltpu.VMEM((4, 1, width), f32), pltpu.VMEM((4, 1, width), f32),
            pltpu.VMEM((4, 1, rows), f32),
            pltpu.VMEM((4, 4, 2, 8, LANES), f32),
            pltpu.SemaphoreType.DMA((4,)),
            pltpu.SemaphoreType.DMA((2, 3, rs_n)), pltpu.SemaphoreType.DMA((2, 3, rs_n)),
            pltpu.SemaphoreType.DMA((8, 3)), pltpu.SemaphoreType.DMA((8, 3)),
            pltpu.SemaphoreType.DMA((2, ag_n + ag_n // 2)), pltpu.SemaphoreType.DMA((2, ag_n + ag_n // 2)),
            pltpu.SemaphoreType.DMA((2, ag_n)),
        ],
        compiler_params=pltpu.CompilerParams(
            collective_id=0, has_side_effects=True, vmem_limit_bytes=40 * 1024 * 1024),
        cost_estimate=pl.CostEstimate(flops=10 * rows * width, bytes_accessed=40 * rows * width, transcendentals=0),
        name="adafactor",
    )(grad_partials, master_weights, row_moment.reshape(1, rows), col_moment.reshape(1, width))
    return (new_master, new_rows.reshape(rows), new_cols.reshape(width), copies, rms.reshape(()))


def solution(mesh):
    return jax.shard_map(
        local,
        mesh=mesh,
        in_specs=(P("dp", None, "row", "col"), P(("dp", "row"), "col"), P(("dp", "row")), P("col")),
        out_specs=(P(("dp", "row"), "col"), P(("dp", "row")), P("col"), P(None, "row", "col"), P()),
        check_vma=False,
    )
```

```python
import functools

import jax
import jax.numpy as jnp
from jax import lax
from jax.experimental import pallas as pl
from jax.experimental.pallas import tpu as pltpu
from jax.sharding import PartitionSpec as P

decay_rate = 0.9
step_rate = 0.05
tiny_value = 1e-30

MESH = pl.DeviceIdType.MESH
LANES = 128
CHUNK = 256
LATE = 1280
AHEAD = 1
AG_ROWS = 16


def kernel(all_rows, full_width, grads, master, row_mom_hbm, col_mom_hbm,
           new_master, new_rows, new_cols, copies, rms_out,
           opp_l, opp_r, add_r, add_l, own_l, own_r, mine, mast, row_mom, col_mom,
           row_part, w_part, col_part, inv_cols, inv_rows, x_buf, y_buf, d_buf, r_buf, f_buf, g_buf,
           load_sem, rs_send, rs_recv, st_send, st_recv, ag_send, ag_recv, ready):
    dp, row, col = lax.axis_index("dp"), lax.axis_index("row"), lax.axis_index("col")
    y, x = row // 4, row % 4
    right, left, far = (dp + 1) % 4, (dp + 3) % 4, (dp + 2) % 4
    rows, width = mine.shape
    half = rows // 2
    strips = rows // 8
    rs_n = width // CHUNK
    early = width - LATE
    early_n = early // CHUNK

    def x_peer(j):
        return {"row": y * 4 + (x + j) % 4}

    def y_peer(j):
        return {"row": ((y + j) % 4) * 4 + x}

    def d_peer(j):
        return {"dp": (dp + j) % 4}

    def c_peer(j):
        return {"col": (col + j) % 4}

    def row_peer(j):
        return {"row": (row + j) % 16}

    def z_peer(j):
        to = (dp * 4 + col + j) % 16
        return {"dp": to // 4, "col": to % 4}

    def signal(sem, peer):
        pl.semaphore_signal(sem, inc=1, device_id=peer, device_id_type=MESH)

    near = [d_peer(1), d_peer(3), x_peer(1), x_peer(3), y_peer(1), y_peer(3), c_peer(1), c_peer(2), c_peer(3)]
    barrier = pltpu.get_barrier_semaphore()
    for peer in near:
        signal(barrier, peer)

    loads = [
        pltpu.make_async_copy(grads.at[0, right, pl.ds(0, half)], add_r, load_sem.at[0]),
        pltpu.make_async_copy(grads.at[0, left, pl.ds(half, half)], add_l, load_sem.at[1]),
        pltpu.make_async_copy(grads.at[0, dp], mine, load_sem.at[2]),
        pltpu.make_async_copy(row_mom_hbm, row_mom, load_sem.at[3]),
        pltpu.make_async_copy(col_mom_hbm, col_mom, load_sem.at[4]),
        pltpu.make_async_copy(master, mast, load_sem.at[5]),
    ]
    for load in loads:
        load.start()
    pl.semaphore_wait(barrier, len(near))

    def rs_copy(way, phase, k):
        to = right if way == 0 else left
        at = pl.ds(pl.multiple_of(k * CHUNK, CHUNK), CHUNK)
        low, high = pl.ds(0, half), pl.ds(half, half)
        mid, other = (low, high) if way == 0 else (high, low)
        opp, own, add = (opp_l, own_l, add_r) if way == 0 else (opp_r, own_r, add_l)
        if phase == 0:
            src, dst = grads.at[0, far, mid, at], opp.at[:, at]
        elif phase == 1:
            src, dst = grads.at[0, to, other, at], own.at[other, at]
        else:
            src, dst = add.at[:, at], own.at[mid, at]
        return pltpu.make_async_remote_copy(
            src_ref=src, dst_ref=dst, send_sem=rs_send.at[way, phase], recv_sem=rs_recv.at[way, min(phase, 1), k],
            device_id={"dp": to}, device_id_type=MESH)

    for k in range(AHEAD):
        rs_copy(0, 0, k).start()
        rs_copy(1, 0, k).start()

    for peer in near:
        signal(ready.at[0], peer)
    row_part[...] = jnp.zeros_like(row_part)
    loads[0].wait()
    loads[1].wait()
    loads[2].wait()
    pl.semaphore_wait(ready.at[0], len(near))
    for j in (1, 2, 3):
        signal(ready.at[1], y_peer(j))
        signal(ready.at[1], d_peer(j))

    def add_strips(add, opp, k):
        at = pl.ds(pl.multiple_of(k * CHUNK, CHUNK), CHUNK)
        for r in range(half // 8):
            down = pl.ds(8 * r, 8)
            add[down, at] = add[down, at] + opp[down, at]

    def take(k):
        at = pl.ds(pl.multiple_of(k * CHUNK, CHUNK), CHUNK)
        for way, own in enumerate((own_l, own_r)):
            pltpu.make_async_copy(own.at[:, at], own.at[:, at], rs_recv.at[way, 1, k]).wait()
        cols = jnp.zeros((8, CHUNK), jnp.float32)
        for r in range(strips):
            down = pl.ds(8 * r, 8)
            g = mine[down, at] + own_l[down, at] + own_r[down, at]
            mine[down, at] = g
            square = g * g
            cols = cols + square
            across = square[:, :LANES]
            for c in range(1, CHUNK // LANES):
                across = across + square[:, c * LANES:(c + 1) * LANES]
            row_part[down] = row_part[down] + across
        col_part[:, at] = jnp.sum(cols, axis=0, keepdims=True)

    def step(k, more=True):
        if more:
            rs_copy(0, 0, k + AHEAD).start()
            rs_copy(1, 0, k + AHEAD).start()
        rs_copy(0, 1, k).start()
        rs_copy(1, 1, k).start()
        rs_copy(0, 0, k).wait_recv()
        add_strips(add_r, opp_l, k)
        rs_copy(0, 2, k).start()
        rs_copy(1, 0, k).wait_recv()
        add_strips(add_l, opp_r, k)
        rs_copy(1, 2, k).start()

    @pl.loop(0, early_n + 2)
    def _(k):
        step(k)

        @pl.when(k >= 2)
        def _():
            take(k - 2)

    pl.semaphore_wait(ready.at[1], 6)

    def stage_copy(stage, buf, me, peer, j):
        return pltpu.make_async_remote_copy(
            src_ref=buf.at[me], dst_ref=buf.at[me], send_sem=st_send.at[stage],
            recv_sem=st_recv.at[stage], device_id=peer(j), device_id_type=MESH)

    stages = ((x_buf, x, x_peer), (y_buf, y, y_peer), (d_buf, dp, d_peer), (r_buf, col, c_peer),
              (f_buf, row, row_peer), (g_buf, dp * 4 + col, z_peer))

    def send(stage, value):
        buf, me, peer = stages[stage]
        buf[me] = value
        for j in range(1, buf.shape[0]):
            stage_copy(stage, buf, me, peer, j).start()

    def receive(stage):
        buf = stages[stage][0]
        others = buf.at[pl.ds(1, buf.shape[0] - 1)]
        pltpu.make_async_copy(others, others, st_recv.at[stage]).wait()

    def total_of(buf, slots):
        values = [buf[s] for s in slots]
        while len(values) > 1:
            values = [a + b for a, b in zip(values[::2], values[1::2])]
        return values[0]

    for k in range(early_n + 2, rs_n):
        if k == early_n + 2:
            send(0, col_part[:, :early])
        elif k == early_n + 3:
            receive(0)
            send(1, total_of(x_buf, range(4)))
        elif k == early_n + 4:
            receive(1)
            send(2, total_of(y_buf, range(4)))
        step(k, k + AHEAD < rs_n)
        take(k - 2)
    receive(2)
    loads[3].wait()
    loads[4].wait()
    next_early = decay_rate * col_mom[:, :early] + (1.0 - decay_rate) * (total_of(d_buf, range(4)) / all_rows + tiny_value)
    new_cols[:, :early] = next_early
    inv_cols[:, :early] = jnp.broadcast_to(1.0 / next_early, (8, early))

    @pl.loop(0, strips)
    def _(r):
        down = pl.ds(pl.multiple_of(r * 8, 8), 8)
        parts = [jnp.zeros((8, LANES), jnp.float32) for _ in range(4)]
        for c in range(early // LANES):
            lanes = pl.ds(c * LANES, LANES)
            g = mine[down, lanes]
            parts[c % 4] = parts[c % 4] + g * g * inv_cols[:, lanes]
        w_part[down] = (parts[0] + parts[1]) + (parts[2] + parts[3])

    for k in range(rs_n - 2, rs_n):
        take(k)

    eye = lax.broadcasted_iota(jnp.int32, (rows, LANES), 0) == lax.broadcasted_iota(jnp.int32, (rows, LANES), 1)
    row_sums = jnp.sum(row_part[...], axis=1, keepdims=True)
    send(3, jnp.sum(jnp.where(eye, row_sums, 0.0), axis=0, keepdims=True))
    share = (decay_rate * col_mom[:, early:] + (1.0 - decay_rate) * tiny_value) / 64.0
    share = share + col_part[:, early:] * ((1.0 - decay_rate) / all_rows)
    receive(3)
    row_mean = total_of(r_buf, range(4)) / full_width + tiny_value
    next_rows = decay_rate * row_mom[...] + (1.0 - decay_rate) * row_mean
    new_rows[...] = next_rows
    rows_down = jnp.sum(jnp.where(eye, next_rows, 0.0), axis=1, keepdims=True)
    inv_rows[...] = jnp.broadcast_to(1.0 / rows_down, inv_rows.shape)

    weighted = []
    for c in range(early // LANES, width // LANES):
        lanes = pl.ds(c * LANES, LANES)
        parts = [jnp.zeros((8, LANES), jnp.float32) for _ in range(2)]
        for r in range(strips):
            down = pl.ds(8 * r, 8)
            g = mine[down, lanes]
            parts[r % 2] = parts[r % 2] + g * g * inv_rows[down]
        weighted.append(jnp.sum(parts[0] + parts[1], axis=0, keepdims=True))
    parts = [jnp.zeros((8, LANES), jnp.float32) for _ in range(2)]
    for r in range(strips):
        down = pl.ds(8 * r, 8)
        parts[r % 2] = parts[r % 2] + w_part[down] * inv_rows[down]
    rest = jnp.sum(parts[0] + parts[1], axis=0, keepdims=True)
    send(4, jnp.concatenate([share] + weighted + [rest, next_rows], axis=1))
    inv_cols[:, :early] = jnp.broadcast_to(lax.rsqrt(new_cols[:, :early]), (8, early))
    inv_rows[...] = jnp.sqrt(inv_rows[...])
    loads[5].wait()
    receive(4)
    send(5, total_of(f_buf, range(16)))
    receive(5)

    squares = jnp.zeros((1, LANES), jnp.float32)
    for c in range(4):
        both = total_of(g_buf, range(c, 16, 4))
        ratio = both[:, LATE:2 * LATE] / both[:, :LATE]
        squares = squares + both[:, 2 * LATE:2 * LATE + LANES]
        for k in range(LATE // LANES):
            squares = squares + ratio[:, k * LANES:(k + 1) * LANES]
        if c == 0:
            scale_mean = jnp.sum(both[:, 2 * LATE + LANES:], axis=(0, 1), keepdims=True) / all_rows
    update_sum = jnp.sum(squares, axis=(0, 1), keepdims=True) * scale_mean
    rms_update = jnp.sqrt(update_sum / (float(all_rows) * float(full_width)))
    rms_out[...] = rms_update
    factor = step_rate * jnp.sqrt(scale_mean) / jnp.maximum(1.0, rms_update)
    next_late = total_of(g_buf.at[:, :, :LATE], [col + 4 * d for d in range(4)])
    new_cols[:, early:] = next_late
    inv_cols[:, early:] = jnp.broadcast_to(lax.rsqrt(next_late), (8, LATE))
    inv_rows[...] = inv_rows[...] * factor

    ag_n = rows // AG_ROWS
    ag_half = ag_n // 2

    def ag_copy(way, k, passed, early=False):
        to = right if way == 0 else left
        at = pl.ds(pl.multiple_of(k * AG_ROWS, AG_ROWS), AG_ROWS)
        slot = (left if way == 0 else right) if passed else dp
        if early:
            sem = k if way == 0 else k - ag_half
        else:
            sem = ag_half
        return pltpu.make_async_remote_copy(
            src_ref=copies.at[slot, at], dst_ref=copies.at[slot, at], send_sem=ag_send.at[way, int(passed)],
            recv_sem=ag_recv.at[way, sem], device_id={"dp": to}, device_id_type=MESH)

    def give(k):
        base = pl.multiple_of(k * AG_ROWS, AG_ROWS)
        at = pl.ds(base, AG_ROWS)
        scale = inv_rows[at]
        for c in range(width // LANES):
            lanes = pl.ds(c * LANES, LANES)
            across = inv_cols[:, lanes]
            across = jnp.concatenate([across] * (AG_ROWS // 8), axis=0)
            w = mast[at, lanes] - mine[at, lanes] * scale * across
            new_master[at, lanes] = w
            copies[dp, at, lanes] = w.astype(jnp.bfloat16)

    @pl.loop(0, ag_half)
    def _(k):
        give(k)
        ag_copy(0, k, False, True).start()
        give(k + ag_half)
        ag_copy(1, k + ag_half, False, True).start()

    @pl.loop(0, ag_half)
    def _(k):
        ag_copy(0, k + ag_half, False).start()
        ag_copy(1, k, False).start()
        ag_copy(0, k, False, True).wait_recv()
        ag_copy(0, k, True).start()
        ag_copy(1, k + ag_half, False, True).wait_recv()
        ag_copy(1, k + ag_half, True).start()

    for way in (0, 1):
        for phase in (0, 1, 2):
            pltpu.make_async_copy(opp_l, opp_l, rs_send.at[way, phase]).wait()
    for stage, (buf, _, _) in enumerate(stages):
        others = buf.at[pl.ds(1, buf.shape[0] - 1)]
        pltpu.make_async_copy(others, others, st_send.at[stage]).wait()
    for way in (0, 1):
        pltpu.make_async_copy(copies.at[dp], copies.at[dp], ag_send.at[way, 0]).wait()
        passed = copies.at[far, pl.ds(0, half)]
        pltpu.make_async_copy(passed, passed, ag_send.at[way, 1]).wait()
        pltpu.make_async_copy(copies.at[far], copies.at[far], ag_recv.at[way, ag_half]).wait()


def write_out(*refs):
    sources, results, sem = refs[:5], refs[5:10], refs[10]
    pieces = [(sources[3].at[d], results[3].at[d]) for d in range(4)]
    half = sources[0].shape[0] // 2
    pieces += [(sources[0].at[pl.ds(h * half, half)], results[0].at[pl.ds(h * half, half)]) for h in range(2)]
    pieces += [(sources[i], results[i]) for i in (1, 2, 4)]
    moves = [pltpu.make_async_copy(a, b, sem.at[i]) for i, (a, b) in enumerate(pieces)]
    for move in moves:
        move.start()
    for move in moves:
        move.wait()


def local(grad_partials, master_weights, row_moment, col_moment):
    rows, width = master_weights.shape
    all_rows = rows * lax.axis_size("dp") * lax.axis_size("row")
    full_width = width * lax.axis_size("col")
    half = rows // 2
    rs_n, ag_n = width // CHUNK, rows // AG_ROWS
    early = width - LATE
    message = 2 * LATE + 2 * LANES
    f32 = jnp.float32
    hbm = pl.BlockSpec(memory_space=pltpu.HBM)
    vmem = pl.BlockSpec(memory_space=pltpu.VMEM)
    results = (
        jax.ShapeDtypeStruct((rows, width), f32),
        jax.ShapeDtypeStruct((1, rows), f32),
        jax.ShapeDtypeStruct((1, width), f32),
        jax.ShapeDtypeStruct((4, rows, width), jnp.bfloat16),
        jax.ShapeDtypeStruct((1, 1), f32),
    )
    held = pl.pallas_call(
        functools.partial(kernel, all_rows, full_width),
        out_shape=results,
        in_specs=[hbm, hbm, hbm, hbm],
        out_specs=(vmem,) * 5,
        scratch_shapes=[
            pltpu.VMEM((half, width), f32), pltpu.VMEM((half, width), f32),
            pltpu.VMEM((half, width), f32), pltpu.VMEM((half, width), f32),
            pltpu.VMEM((rows, width), f32), pltpu.VMEM((rows, width), f32),
            pltpu.VMEM((rows, width), f32), pltpu.VMEM((rows, width), f32),
            pltpu.VMEM((1, rows), f32), pltpu.VMEM((1, width), f32),
            pltpu.VMEM((rows, LANES), f32), pltpu.VMEM((rows, LANES), f32),
            pltpu.VMEM((1, width), f32), pltpu.VMEM((8, width), f32),
            pltpu.VMEM((rows, LANES), f32),
            pltpu.VMEM((4, 1, early), f32), pltpu.VMEM((4, 1, early), f32), pltpu.VMEM((4, 1, early), f32),
            pltpu.VMEM((4, 1, rows), f32),
            pltpu.VMEM((16, 1, message), f32), pltpu.VMEM((16, 1, message), f32),
            pltpu.SemaphoreType.DMA((6,)),
            pltpu.SemaphoreType.DMA((2, 3)), pltpu.SemaphoreType.DMA((2, 2, rs_n)),
            pltpu.SemaphoreType.DMA((6,)), pltpu.SemaphoreType.DMA((6,)),
            pltpu.SemaphoreType.DMA((2, 2)), pltpu.SemaphoreType.DMA((2, ag_n // 2 + 1)),
            pltpu.SemaphoreType.REGULAR((2,)),
        ],
        compiler_params=pltpu.CompilerParams(
            collective_id=0, has_side_effects=True, vmem_limit_bytes=40 * 1024 * 1024),
        cost_estimate=pl.CostEstimate(flops=10 * rows * width, bytes_accessed=40 * rows * width, transcendentals=0),
        name="adafactor",
    )(*[pltpu.with_memory_space_constraint(a, pltpu.HBM) for a in (grad_partials, master_weights, row_moment.reshape(1, rows), col_moment.reshape(1, width))])
    new_master, new_rows, new_cols, copies, rms = pl.pallas_call(
        write_out,
        out_shape=results,
        in_specs=[pl.BlockSpec(memory_space=pl.ANY)] * 5,
        out_specs=(hbm,) * 5,
        scratch_shapes=[pltpu.SemaphoreType.DMA((9,))],
        compiler_params=pltpu.CompilerParams(vmem_limit_bytes=1024 * 1024),
        cost_estimate=pl.CostEstimate(flops=0, bytes_accessed=24 * rows * width, transcendentals=0),
        name="write_out",
    )(*[pltpu.with_memory_space_constraint(a, pltpu.VMEM) for a in held])
    return (new_master, new_rows.reshape(rows), new_cols.reshape(width), copies, rms.reshape(()))


def solution(mesh):
    return jax.shard_map(
        local,
        mesh=mesh,
        in_specs=(P("dp", None, "row", "col"), P(("dp", "row"), "col"), P(("dp", "row")), P("col")),
        out_specs=(P(("dp", "row"), "col"), P(("dp", "row")), P("col"), P(None, "row", "col"), P()),
        check_vma=False,
    )
```

```python
import functools

import jax
import jax.numpy as jnp
from jax import lax
from jax.experimental import pallas as pl
from jax.experimental.pallas import tpu as pltpu
from jax.sharding import PartitionSpec as P

decay_rate = 0.9
step_rate = 0.05
tiny_value = 1e-30

MESH = pl.DeviceIdType.MESH
LANES = 128
CHUNK = 256
LATE = 768
AHEAD = 1
AG_ROWS = 16


def kernel(all_rows, full_width, grads, master, row_mom_hbm, col_mom_hbm,
           new_master, new_rows, new_cols, copies, rms_out,
           opp_l, opp_r, add_r, add_l, own_l, own_r, mine, mast, row_mom, col_mom,
           row_part, w_part, col_part, inv_cols, inv_rows, x_buf, y_buf, d_buf, r_buf, f_buf, g_buf,
           load_sem, rs_send, rs_recv, st_send, st_recv, ag_send, ag_recv, ready):
    dp, row, col = lax.axis_index("dp"), lax.axis_index("row"), lax.axis_index("col")
    y, x = row // 4, row % 4
    right, left, far = (dp + 1) % 4, (dp + 3) % 4, (dp + 2) % 4
    rows, width = mine.shape
    half = rows // 2
    strips = rows // 8
    rs_n = width // CHUNK
    early = width - LATE
    early_n = early // CHUNK

    def x_peer(j):
        return {"row": y * 4 + (x + j) % 4}

    def y_peer(j):
        return {"row": ((y + j) % 4) * 4 + x}

    def d_peer(j):
        return {"dp": (dp + j) % 4}

    def c_peer(j):
        return {"col": (col + j) % 4}

    def row_peer(j):
        return {"row": (row + j) % 16}

    def z_peer(j):
        to = (dp * 4 + col + j) % 16
        return {"dp": to // 4, "col": to % 4}

    def signal(sem, peer):
        pl.semaphore_signal(sem, inc=1, device_id=peer, device_id_type=MESH)

    near = [d_peer(1), d_peer(3), x_peer(1), y_peer(1), c_peer(1)]
    back = [x_peer(3), y_peer(3), c_peer(3)]
    barrier = pltpu.get_barrier_semaphore()
    for peer in near:
        signal(barrier, peer)

    loads = [
        pltpu.make_async_copy(grads.at[0, right, pl.ds(0, half)], add_r, load_sem.at[0]),
        pltpu.make_async_copy(grads.at[0, left, pl.ds(half, half)], add_l, load_sem.at[1]),
        pltpu.make_async_copy(grads.at[0, dp], mine, load_sem.at[2]),
        pltpu.make_async_copy(row_mom_hbm, row_mom, load_sem.at[3]),
        pltpu.make_async_copy(col_mom_hbm, col_mom, load_sem.at[4]),
        pltpu.make_async_copy(master, mast, load_sem.at[5]),
    ]
    for load in loads:
        load.start()
    pl.semaphore_wait(barrier, len(near))

    def rs_copy(way, phase, k):
        to = right if way == 0 else left
        at = pl.ds(pl.multiple_of(k * CHUNK, CHUNK), CHUNK)
        low, high = pl.ds(0, half), pl.ds(half, half)
        mid, other = (low, high) if way == 0 else (high, low)
        opp, own, add = (opp_l, own_l, add_r) if way == 0 else (opp_r, own_r, add_l)
        if phase == 0:
            src, dst = grads.at[0, far, mid, at], opp.at[:, at]
        elif phase == 1:
            src, dst = grads.at[0, to, other, at], own.at[other, at]
        else:
            src, dst = add.at[:, at], own.at[mid, at]
        return pltpu.make_async_remote_copy(
            src_ref=src, dst_ref=dst, send_sem=rs_send.at[way, phase], recv_sem=rs_recv.at[way, min(phase, 1), k],
            device_id={"dp": to}, device_id_type=MESH)

    for k in range(AHEAD):
        rs_copy(0, 0, k).start()
        rs_copy(1, 0, k).start()

    for peer in back:
        signal(ready.at[0], peer)
    row_part[...] = jnp.zeros_like(row_part)
    loads[0].wait()
    loads[1].wait()
    loads[2].wait()
    pl.semaphore_wait(ready.at[0], len(back))
    for peer in back:
        signal(ready.at[1], peer)

    def add_strips(add, opp, k):
        at = pl.ds(pl.multiple_of(k * CHUNK, CHUNK), CHUNK)
        for r in range(half // 8):
            down = pl.ds(8 * r, 8)
            add[down, at] = add[down, at] + opp[down, at]

    def take(k):
        at = pl.ds(pl.multiple_of(k * CHUNK, CHUNK), CHUNK)
        for way, own in enumerate((own_l, own_r)):
            pltpu.make_async_copy(own.at[:, at], own.at[:, at], rs_recv.at[way, 1, k]).wait()
        cols = jnp.zeros((8, CHUNK), jnp.float32)
        for r in range(strips):
            down = pl.ds(8 * r, 8)
            g = mine[down, at] + own_l[down, at] + own_r[down, at]
            mine[down, at] = g
            square = g * g
            cols = cols + square
            across = square[:, :LANES]
            for c in range(1, CHUNK // LANES):
                across = across + square[:, c * LANES:(c + 1) * LANES]
            row_part[down] = row_part[down] + across
        col_part[:, at] = jnp.sum(cols, axis=0, keepdims=True)

    def issue(k, more=True):
        if more:
            rs_copy(0, 0, k + AHEAD).start()
            rs_copy(1, 0, k + AHEAD).start()
        rs_copy(0, 1, k).start()
        rs_copy(1, 1, k).start()

    def pass_on(k):
        rs_copy(0, 0, k).wait_recv()
        add_strips(add_r, opp_l, k)
        rs_copy(0, 2, k).start()
        rs_copy(1, 0, k).wait_recv()
        add_strips(add_l, opp_r, k)
        rs_copy(1, 2, k).start()

    @pl.loop(0, early_n + 1)
    def _(k):
        issue(k)

        @pl.when(k >= 2)
        def _():
            take(k - 2)

        pass_on(k)

        @pl.when(k == 4)
        def _():
            pl.semaphore_wait(ready.at[1], len(back))
            for j in (1, 2, 3):
                signal(ready.at[2], y_peer(j))
                signal(ready.at[2], d_peer(j))

        @pl.when(k == 8)
        def _():
            pl.semaphore_wait(ready.at[2], 6)

    def stage_copy(stage, buf, me, peer, j):
        return pltpu.make_async_remote_copy(
            src_ref=buf.at[me], dst_ref=buf.at[me], send_sem=st_send.at[stage],
            recv_sem=st_recv.at[stage], device_id=peer(j), device_id_type=MESH)

    stages = ((x_buf, x, x_peer), (y_buf, y, y_peer), (d_buf, dp, d_peer), (r_buf, col, c_peer),
              (f_buf, row, row_peer), (g_buf, dp * 4 + col, z_peer))

    def send(stage, value):
        buf, me, peer = stages[stage]
        buf[me] = value
        for j in range(1, buf.shape[0]):
            stage_copy(stage, buf, me, peer, j).start()

    def receive(stage):
        buf = stages[stage][0]
        others = buf.at[pl.ds(1, buf.shape[0] - 1)]
        pltpu.make_async_copy(others, others, st_recv.at[stage]).wait()

    def total_of(buf, slots):
        values = [buf[s] for s in slots]
        while len(values) > 1:
            values = [a + b for a, b in zip(values[::2], values[1::2])]
        return values[0]

    for k in range(early_n + 1, rs_n):
        if k == early_n + 2:
            receive(0)
            send(1, total_of(x_buf, range(4)))
            receive(1)
            send(2, total_of(y_buf, range(4)))
        issue(k, k + AHEAD < rs_n)
        take(k - 2)
        if k == early_n + 1:
            send(0, col_part[:, :early])
        pass_on(k)
    receive(2)
    loads[3].wait()
    loads[4].wait()
    next_early = decay_rate * col_mom[:, :early] + (1.0 - decay_rate) * (total_of(d_buf, range(4)) / all_rows + tiny_value)
    new_cols[:, :early] = next_early
    inv_cols[:, :early] = jnp.broadcast_to(1.0 / next_early, (8, early))

    @pl.loop(0, strips)
    def _(r):
        down = pl.ds(pl.multiple_of(r * 8, 8), 8)
        parts = [jnp.zeros((8, LANES), jnp.float32) for _ in range(4)]
        for c in range(early // LANES):
            lanes = pl.ds(c * LANES, LANES)
            g = mine[down, lanes]
            parts[c % 4] = parts[c % 4] + g * g * inv_cols[:, lanes]
        w_part[down] = (parts[0] + parts[1]) + (parts[2] + parts[3])

    for k in range(rs_n - 2, rs_n):
        take(k)

    eye = lax.broadcasted_iota(jnp.int32, (rows, LANES), 0) == lax.broadcasted_iota(jnp.int32, (rows, LANES), 1)
    row_sums = jnp.sum(row_part[...], axis=1, keepdims=True)
    send(3, jnp.sum(jnp.where(eye, row_sums, 0.0), axis=0, keepdims=True))
    share = (decay_rate * col_mom[:, early:] + (1.0 - decay_rate) * tiny_value) / 64.0
    share = share + col_part[:, early:] * ((1.0 - decay_rate) / all_rows)
    receive(3)
    row_mean = total_of(r_buf, range(4)) / full_width + tiny_value
    next_rows = decay_rate * row_mom[...] + (1.0 - decay_rate) * row_mean
    new_rows[...] = next_rows
    rows_down = jnp.sum(jnp.where(eye, next_rows, 0.0), axis=1, keepdims=True)
    inv_rows[...] = jnp.broadcast_to(1.0 / rows_down, inv_rows.shape)

    weighted = []
    for c in range(early // LANES, width // LANES):
        lanes = pl.ds(c * LANES, LANES)
        parts = [jnp.zeros((8, LANES), jnp.float32) for _ in range(2)]
        for r in range(strips):
            down = pl.ds(8 * r, 8)
            g = mine[down, lanes]
            parts[r % 2] = parts[r % 2] + g * g * inv_rows[down]
        weighted.append(jnp.sum(parts[0] + parts[1], axis=0, keepdims=True))
    parts = [jnp.zeros((8, LANES), jnp.float32) for _ in range(2)]
    for r in range(strips):
        down = pl.ds(8 * r, 8)
        parts[r % 2] = parts[r % 2] + w_part[down] * inv_rows[down]
    rest = jnp.sum(parts[0] + parts[1], axis=0, keepdims=True)
    send(4, jnp.concatenate([share] + weighted + [rest, next_rows], axis=1))
    inv_cols[:, :early] = jnp.broadcast_to(lax.rsqrt(new_cols[:, :early]), (8, early))
    inv_rows[...] = jnp.sqrt(inv_rows[...])
    loads[5].wait()
    receive(4)
    send(5, total_of(f_buf, range(16)))
    receive(5)

    squares = jnp.zeros((1, LANES), jnp.float32)
    for c in range(4):
        both = total_of(g_buf, range(c, 16, 4))
        ratio = both[:, LATE:2 * LATE] / both[:, :LATE]
        squares = squares + both[:, 2 * LATE:2 * LATE + LANES]
        for k in range(LATE // LANES):
            squares = squares + ratio[:, k * LANES:(k + 1) * LANES]
        if c == 0:
            scale_mean = jnp.sum(both[:, 2 * LATE + LANES:], axis=(0, 1), keepdims=True) / all_rows
    update_sum = jnp.sum(squares, axis=(0, 1), keepdims=True) * scale_mean
    rms_update = jnp.sqrt(update_sum / (float(all_rows) * float(full_width)))
    rms_out[...] = rms_update
    factor = step_rate * jnp.sqrt(scale_mean) / jnp.maximum(1.0, rms_update)
    next_late = total_of(g_buf.at[:, :, :LATE], [col + 4 * d for d in range(4)])
    new_cols[:, early:] = next_late
    inv_cols[:, early:] = jnp.broadcast_to(lax.rsqrt(next_late), (8, LATE))
    inv_rows[...] = inv_rows[...] * factor

    ag_n = rows // AG_ROWS
    ag_half = ag_n // 2

    def ag_copy(way, k, passed, early=False):
        to = right if way == 0 else left
        at = pl.ds(pl.multiple_of(k * AG_ROWS, AG_ROWS), AG_ROWS)
        slot = (left if way == 0 else right) if passed else dp
        if early:
            sem = k if way == 0 else k - ag_half
        else:
            sem = ag_half
        return pltpu.make_async_remote_copy(
            src_ref=copies.at[slot, at], dst_ref=copies.at[slot, at], send_sem=ag_send.at[way, int(passed)],
            recv_sem=ag_recv.at[way, sem], device_id={"dp": to}, device_id_type=MESH)

    def give(k):
        base = pl.multiple_of(k * AG_ROWS, AG_ROWS)
        at = pl.ds(base, AG_ROWS)
        scale = inv_rows[at]
        for c in range(width // LANES):
            lanes = pl.ds(c * LANES, LANES)
            across = inv_cols[:, lanes]
            across = jnp.concatenate([across] * (AG_ROWS // 8), axis=0)
            w = mast[at, lanes] - mine[at, lanes] * scale * across
            new_master[at, lanes] = w
            copies[dp, at, lanes] = w.astype(jnp.bfloat16)

    @pl.loop(0, ag_half)
    def _(k):
        give(k)
        ag_copy(0, k, False, True).start()
        give(k + ag_half)
        ag_copy(1, k + ag_half, False, True).start()

    @pl.loop(0, ag_half)
    def _(k):
        ag_copy(0, k + ag_half, False).start()
        ag_copy(1, k, False).start()
        ag_copy(0, k, False, True).wait_recv()
        ag_copy(0, k, True).start()
        ag_copy(1, k + ag_half, False, True).wait_recv()
        ag_copy(1, k + ag_half, True).start()

    for way in (0, 1):
        for phase in (0, 1, 2):
            pltpu.make_async_copy(opp_l, opp_l, rs_send.at[way, phase]).wait()
    for stage, (buf, _, _) in enumerate(stages):
        others = buf.at[pl.ds(1, buf.shape[0] - 1)]
        pltpu.make_async_copy(others, others, st_send.at[stage]).wait()
    for way in (0, 1):
        pltpu.make_async_copy(copies.at[dp], copies.at[dp], ag_send.at[way, 0]).wait()
        passed = copies.at[far, pl.ds(0, half)]
        pltpu.make_async_copy(passed, passed, ag_send.at[way, 1]).wait()
        pltpu.make_async_copy(copies.at[far], copies.at[far], ag_recv.at[way, ag_half]).wait()


def write_out(*refs):
    sources, results, sem = refs[:5], refs[5:10], refs[10]
    pieces = [(sources[3].at[d], results[3].at[d]) for d in range(4)]
    half = sources[0].shape[0] // 2
    pieces += [(sources[0].at[pl.ds(h * half, half)], results[0].at[pl.ds(h * half, half)]) for h in range(2)]
    pieces += [(sources[i], results[i]) for i in (1, 2, 4)]
    moves = [pltpu.make_async_copy(a, b, sem.at[i]) for i, (a, b) in enumerate(pieces)]
    for move in moves:
        move.start()
    for move in moves:
        move.wait()


def local(grad_partials, master_weights, row_moment, col_moment):
    rows, width = master_weights.shape
    all_rows = rows * lax.axis_size("dp") * lax.axis_size("row")
    full_width = width * lax.axis_size("col")
    half = rows // 2
    rs_n, ag_n = width // CHUNK, rows // AG_ROWS
    early = width - LATE
    message = 2 * LATE + 2 * LANES
    f32 = jnp.float32
    hbm = pl.BlockSpec(memory_space=pltpu.HBM)
    vmem = pl.BlockSpec(memory_space=pltpu.VMEM)
    results = (
        jax.ShapeDtypeStruct((rows, width), f32),
        jax.ShapeDtypeStruct((1, rows), f32),
        jax.ShapeDtypeStruct((1, width), f32),
        jax.ShapeDtypeStruct((4, rows, width), jnp.bfloat16),
        jax.ShapeDtypeStruct((1, 1), f32),
    )
    held = pl.pallas_call(
        functools.partial(kernel, all_rows, full_width),
        out_shape=results,
        in_specs=[hbm, hbm, hbm, hbm],
        out_specs=(vmem,) * 5,
        scratch_shapes=[
            pltpu.VMEM((half, width), f32), pltpu.VMEM((half, width), f32),
            pltpu.VMEM((half, width), f32), pltpu.VMEM((half, width), f32),
            pltpu.VMEM((rows, width), f32), pltpu.VMEM((rows, width), f32),
            pltpu.VMEM((rows, width), f32), pltpu.VMEM((rows, width), f32),
            pltpu.VMEM((1, rows), f32), pltpu.VMEM((1, width), f32),
            pltpu.VMEM((rows, LANES), f32), pltpu.VMEM((rows, LANES), f32),
            pltpu.VMEM((1, width), f32), pltpu.VMEM((8, width), f32),
            pltpu.VMEM((rows, LANES), f32),
            pltpu.VMEM((4, 1, early), f32), pltpu.VMEM((4, 1, early), f32), pltpu.VMEM((4, 1, early), f32),
            pltpu.VMEM((4, 1, rows), f32),
            pltpu.VMEM((16, 1, message), f32), pltpu.VMEM((16, 1, message), f32),
            pltpu.SemaphoreType.DMA((6,)),
            pltpu.SemaphoreType.DMA((2, 3)), pltpu.SemaphoreType.DMA((2, 2, rs_n)),
            pltpu.SemaphoreType.DMA((6,)), pltpu.SemaphoreType.DMA((6,)),
            pltpu.SemaphoreType.DMA((2, 2)), pltpu.SemaphoreType.DMA((2, ag_n // 2 + 1)),
            pltpu.SemaphoreType.REGULAR((3,)),
        ],
        compiler_params=pltpu.CompilerParams(
            collective_id=0, has_side_effects=True, vmem_limit_bytes=40 * 1024 * 1024),
        cost_estimate=pl.CostEstimate(flops=10 * rows * width, bytes_accessed=40 * rows * width, transcendentals=0),
        name="adafactor",
    )(*[pltpu.with_memory_space_constraint(a, pltpu.HBM) for a in (grad_partials, master_weights, row_moment.reshape(1, rows), col_moment.reshape(1, width))])
    new_master, new_rows, new_cols, copies, rms = pl.pallas_call(
        write_out,
        out_shape=results,
        in_specs=[pl.BlockSpec(memory_space=pl.ANY)] * 5,
        out_specs=(hbm,) * 5,
        scratch_shapes=[pltpu.SemaphoreType.DMA((9,))],
        compiler_params=pltpu.CompilerParams(vmem_limit_bytes=1024 * 1024),
        cost_estimate=pl.CostEstimate(flops=0, bytes_accessed=24 * rows * width, transcendentals=0),
        name="write_out",
    )(*[pltpu.with_memory_space_constraint(a, pltpu.VMEM) for a in held])
    return (new_master, new_rows.reshape(rows), new_cols.reshape(width), copies, rms.reshape(()))


def solution(mesh):
    return jax.shard_map(
        local,
        mesh=mesh,
        in_specs=(P("dp", None, "row", "col"), P(("dp", "row"), "col"), P(("dp", "row")), P("col")),
        out_specs=(P(("dp", "row"), "col"), P(("dp", "row")), P("col"), P(None, "row", "col"), P()),
        check_vma=False,
    )
```

```python
import functools

import jax
import jax.numpy as jnp
from jax import lax
from jax.experimental import pallas as pl
from jax.experimental.pallas import tpu as pltpu
from jax.sharding import PartitionSpec as P

decay_rate = 0.9
step_rate = 0.05
tiny_value = 1e-30

MESH = pl.DeviceIdType.MESH
LANES = 128
CHUNK = 256
LATE = 768
AHEAD = 1
AG_ROWS = 16


def kernel(all_rows, full_width, grads, master, row_mom_hbm, col_mom_hbm,
           new_master, new_rows, new_cols, copies, rms_out,
           opp_l, opp_r, add_r, add_l, own_l, own_r, mine, mast, row_mom, col_mom,
           row_part, w_part, col_part, inv_cols, inv_rows, x_buf, y_buf, d_buf, r_buf, f_buf, g_buf, h_buf,
           load_sem, rs_send, rs_recv, st_send, st_recv, ag_send, ag_recv, ready):
    dp, row, col = lax.axis_index("dp"), lax.axis_index("row"), lax.axis_index("col")
    y, x = row // 4, row % 4
    right, left, far = (dp + 1) % 4, (dp + 3) % 4, (dp + 2) % 4
    rows, width = mine.shape
    half = rows // 2
    strips = rows // 8
    rs_n = width // CHUNK
    early = width - LATE
    early_n = early // CHUNK

    def x_peer(j):
        return {"row": y * 4 + (x + j) % 4}

    def y_peer(j):
        return {"row": ((y + j) % 4) * 4 + x}

    def d_peer(j):
        return {"dp": (dp + j) % 4}

    def c_peer(j):
        return {"col": (col + j) % 4}

    def row_peer(j):
        return {"row": (row + j) % 16}

    def z_peer(j):
        to = (dp * 4 + col + j) % 16
        return {"dp": to // 4, "col": to % 4}

    def signal(sem, peer):
        pl.semaphore_signal(sem, inc=1, device_id=peer, device_id_type=MESH)

    near = [d_peer(1), d_peer(3), x_peer(1), y_peer(1), c_peer(1)]
    back = [x_peer(3), y_peer(3), c_peer(3)]
    barrier = pltpu.get_barrier_semaphore()
    for peer in near:
        signal(barrier, peer)

    loads = [
        pltpu.make_async_copy(grads.at[0, right, pl.ds(0, half)], add_r, load_sem.at[0]),
        pltpu.make_async_copy(grads.at[0, left, pl.ds(half, half)], add_l, load_sem.at[1]),
        pltpu.make_async_copy(grads.at[0, dp], mine, load_sem.at[2]),
        pltpu.make_async_copy(row_mom_hbm, row_mom, load_sem.at[3]),
        pltpu.make_async_copy(col_mom_hbm, col_mom, load_sem.at[4]),
        pltpu.make_async_copy(master, mast, load_sem.at[5]),
    ]
    for load in loads:
        load.start()
    pl.semaphore_wait(barrier, len(near))

    def rs_copy(way, phase, k):
        to = right if way == 0 else left
        at = pl.ds(pl.multiple_of(k * CHUNK, CHUNK), CHUNK)
        low, high = pl.ds(0, half), pl.ds(half, half)
        mid, other = (low, high) if way == 0 else (high, low)
        opp, own, add = (opp_l, own_l, add_r) if way == 0 else (opp_r, own_r, add_l)
        if phase == 0:
            src, dst = grads.at[0, far, mid, at], opp.at[:, at]
        elif phase == 1:
            src, dst = grads.at[0, to, other, at], own.at[other, at]
        else:
            src, dst = add.at[:, at], own.at[mid, at]
        return pltpu.make_async_remote_copy(
            src_ref=src, dst_ref=dst, send_sem=rs_send.at[way, phase], recv_sem=rs_recv.at[way, min(phase, 1), k],
            device_id={"dp": to}, device_id_type=MESH)

    for k in range(AHEAD):
        rs_copy(0, 0, k).start()
        rs_copy(1, 0, k).start()

    for peer in back:
        signal(ready.at[0], peer)
    row_part[...] = jnp.zeros_like(row_part)
    loads[0].wait()
    loads[1].wait()
    loads[2].wait()
    pl.semaphore_wait(ready.at[0], len(back))
    for peer in back:
        signal(ready.at[1], peer)

    def add_strips(add, opp, k):
        at = pl.ds(pl.multiple_of(k * CHUNK, CHUNK), CHUNK)
        for r in range(half // 8):
            down = pl.ds(8 * r, 8)
            add[down, at] = add[down, at] + opp[down, at]

    def take(k):
        at = pl.ds(pl.multiple_of(k * CHUNK, CHUNK), CHUNK)
        for way, own in enumerate((own_l, own_r)):
            pltpu.make_async_copy(own.at[:, at], own.at[:, at], rs_recv.at[way, 1, k]).wait()
        cols = jnp.zeros((8, CHUNK), jnp.float32)
        for r in range(strips):
            down = pl.ds(8 * r, 8)
            g = mine[down, at] + own_l[down, at] + own_r[down, at]
            mine[down, at] = g
            square = g * g
            cols = cols + square
            across = square[:, :LANES]
            for c in range(1, CHUNK // LANES):
                across = across + square[:, c * LANES:(c + 1) * LANES]
            row_part[down] = row_part[down] + across
        col_part[:, at] = jnp.sum(cols, axis=0, keepdims=True)

    def issue(k, more=True):
        if more:
            rs_copy(0, 0, k + AHEAD).start()
            rs_copy(1, 0, k + AHEAD).start()
        rs_copy(0, 1, k).start()
        rs_copy(1, 1, k).start()

    def pass_on(k):
        rs_copy(0, 0, k).wait_recv()
        add_strips(add_r, opp_l, k)
        rs_copy(0, 2, k).start()
        rs_copy(1, 0, k).wait_recv()
        add_strips(add_l, opp_r, k)
        rs_copy(1, 2, k).start()

    @pl.loop(0, early_n + 1)
    def _(k):
        issue(k)

        @pl.when(k >= 2)
        def _():
            take(k - 2)

        pass_on(k)

        @pl.when(k == 4)
        def _():
            pl.semaphore_wait(ready.at[1], len(back))
            for j in (1, 2, 3):
                signal(ready.at[2], y_peer(j))
                signal(ready.at[2], d_peer(j))

        @pl.when(k == 8)
        def _():
            pl.semaphore_wait(ready.at[2], 6)

    def stage_copy(stage, buf, me, peer, j):
        return pltpu.make_async_remote_copy(
            src_ref=buf.at[me], dst_ref=buf.at[me], send_sem=st_send.at[stage],
            recv_sem=st_recv.at[stage], device_id=peer(j), device_id_type=MESH)

    stages = ((x_buf, x, x_peer), (y_buf, y, y_peer), (d_buf, dp, d_peer), (r_buf, col, c_peer),
              (f_buf, row, row_peer), (g_buf, dp, d_peer), (h_buf, col, c_peer))

    def send(stage, value):
        buf, me, peer = stages[stage]
        buf[me] = value
        for j in range(1, buf.shape[0]):
            stage_copy(stage, buf, me, peer, j).start()

    def receive(stage):
        buf = stages[stage][0]
        others = buf.at[pl.ds(1, buf.shape[0] - 1)]
        pltpu.make_async_copy(others, others, st_recv.at[stage]).wait()

    def total_of(buf, slots):
        values = [buf[s] for s in slots]
        while len(values) > 1:
            values = [a + b for a, b in zip(values[::2], values[1::2])]
        return values[0]

    for k in range(early_n + 1, rs_n):
        if k == early_n + 2:
            receive(0)
            send(1, total_of(x_buf, range(4)))
            receive(1)
            send(2, total_of(y_buf, range(4)))
        issue(k, k + AHEAD < rs_n)
        take(k - 2)
        if k == early_n + 1:
            send(0, col_part[:, :early])
        pass_on(k)
    for k in range(rs_n - 2, rs_n):
        take(k)

    eye = lax.broadcasted_iota(jnp.int32, (rows, LANES), 0) == lax.broadcasted_iota(jnp.int32, (rows, LANES), 1)
    row_sums = jnp.sum(row_part[...], axis=1, keepdims=True)
    send(3, jnp.sum(jnp.where(eye, row_sums, 0.0), axis=0, keepdims=True))
    receive(2)
    loads[3].wait()
    loads[4].wait()
    next_early = decay_rate * col_mom[:, :early] + (1.0 - decay_rate) * (total_of(d_buf, range(4)) / all_rows + tiny_value)
    new_cols[:, :early] = next_early
    inv_cols[:, :early] = jnp.broadcast_to(1.0 / next_early, (8, early))

    @pl.loop(0, strips)
    def _(r):
        down = pl.ds(pl.multiple_of(r * 8, 8), 8)
        parts = [jnp.zeros((8, LANES), jnp.float32) for _ in range(4)]
        for c in range(early // LANES):
            lanes = pl.ds(c * LANES, LANES)
            g = mine[down, lanes]
            parts[c % 4] = parts[c % 4] + g * g * inv_cols[:, lanes]
        w_part[down] = (parts[0] + parts[1]) + (parts[2] + parts[3])

    share = (decay_rate * col_mom[:, early:] + (1.0 - decay_rate) * tiny_value) / 64.0
    share = share + col_part[:, early:] * ((1.0 - decay_rate) / all_rows)
    receive(3)
    row_mean = total_of(r_buf, range(4)) / full_width + tiny_value
    next_rows = decay_rate * row_mom[...] + (1.0 - decay_rate) * row_mean
    new_rows[...] = next_rows
    rows_down = jnp.sum(jnp.where(eye, next_rows, 0.0), axis=1, keepdims=True)
    inv_rows[...] = jnp.broadcast_to(1.0 / rows_down, inv_rows.shape)

    weighted = []
    for c in range(early // LANES, width // LANES):
        lanes = pl.ds(c * LANES, LANES)
        parts = [jnp.zeros((8, LANES), jnp.float32) for _ in range(2)]
        for r in range(strips):
            down = pl.ds(8 * r, 8)
            g = mine[down, lanes]
            parts[r % 2] = parts[r % 2] + g * g * inv_rows[down]
        weighted.append(jnp.sum(parts[0] + parts[1], axis=0, keepdims=True))
    parts = [jnp.zeros((8, LANES), jnp.float32) for _ in range(2)]
    for r in range(strips):
        down = pl.ds(8 * r, 8)
        parts[r % 2] = parts[r % 2] + w_part[down] * inv_rows[down]
    rest = jnp.sum(parts[0] + parts[1], axis=0, keepdims=True)
    send(4, jnp.concatenate([share] + weighted + [rest, next_rows], axis=1))
    inv_cols[:, :early] = jnp.broadcast_to(lax.rsqrt(new_cols[:, :early]), (8, early))
    inv_rows[...] = jnp.sqrt(inv_rows[...])
    loads[5].wait()
    receive(4)
    send(5, total_of(f_buf, range(16)))
    receive(5)
    both = total_of(g_buf, range(4))
    next_late = both[:, :LATE]
    ratio = both[:, LATE:2 * LATE] / next_late
    squares = both[:, 2 * LATE:2 * LATE + LANES]
    for c in range(LATE // LANES):
        squares = squares + ratio[:, c * LANES:(c + 1) * LANES]
    send(6, squares)
    scale_mean = jnp.sum(both[:, 2 * LATE + LANES:], axis=(0, 1), keepdims=True) / all_rows
    new_cols[:, early:] = next_late
    inv_cols[:, early:] = jnp.broadcast_to(lax.rsqrt(next_late), (8, LATE))
    receive(6)
    squares = total_of(h_buf, range(4))
    update_sum = jnp.sum(squares, axis=(0, 1), keepdims=True) * scale_mean
    rms_update = jnp.sqrt(update_sum / (float(all_rows) * float(full_width)))
    rms_out[...] = rms_update
    factor = step_rate * jnp.sqrt(scale_mean) / jnp.maximum(1.0, rms_update)
    inv_rows[...] = inv_rows[...] * factor

    ag_n = rows // AG_ROWS
    ag_half = ag_n // 2

    def ag_copy(way, k, passed, early=False):
        to = right if way == 0 else left
        at = pl.ds(pl.multiple_of(k * AG_ROWS, AG_ROWS), AG_ROWS)
        slot = (left if way == 0 else right) if passed else dp
        if early:
            sem = k if way == 0 else k - ag_half
        else:
            sem = ag_half
        return pltpu.make_async_remote_copy(
            src_ref=copies.at[slot, at], dst_ref=copies.at[slot, at], send_sem=ag_send.at[way, int(passed)],
            recv_sem=ag_recv.at[way, sem], device_id={"dp": to}, device_id_type=MESH)

    def give(k):
        base = pl.multiple_of(k * AG_ROWS, AG_ROWS)
        at = pl.ds(base, AG_ROWS)
        scale = inv_rows[at]
        for c in range(width // LANES):
            lanes = pl.ds(c * LANES, LANES)
            across = inv_cols[:, lanes]
            across = jnp.concatenate([across] * (AG_ROWS // 8), axis=0)
            w = mast[at, lanes] - mine[at, lanes] * scale * across
            new_master[at, lanes] = w
            copies[dp, at, lanes] = w.astype(jnp.bfloat16)

    @pl.loop(0, ag_half)
    def _(k):
        give(k)
        ag_copy(0, k, False, True).start()
        give(k + ag_half)
        ag_copy(1, k + ag_half, False, True).start()

    @pl.loop(0, ag_half)
    def _(k):
        ag_copy(0, k + ag_half, False).start()
        ag_copy(1, k, False).start()
        ag_copy(0, k, False, True).wait_recv()
        ag_copy(0, k, True).start()
        ag_copy(1, k + ag_half, False, True).wait_recv()
        ag_copy(1, k + ag_half, True).start()

    for way in (0, 1):
        for phase in (0, 1, 2):
            pltpu.make_async_copy(opp_l, opp_l, rs_send.at[way, phase]).wait()
    for stage, (buf, _, _) in enumerate(stages):
        others = buf.at[pl.ds(1, buf.shape[0] - 1)]
        pltpu.make_async_copy(others, others, st_send.at[stage]).wait()
    for way in (0, 1):
        pltpu.make_async_copy(copies.at[dp], copies.at[dp], ag_send.at[way, 0]).wait()
        passed = copies.at[far, pl.ds(0, half)]
        pltpu.make_async_copy(passed, passed, ag_send.at[way, 1]).wait()
        pltpu.make_async_copy(copies.at[far], copies.at[far], ag_recv.at[way, ag_half]).wait()


def write_out(*refs):
    sources, results, sem = refs[:5], refs[5:10], refs[10]
    pieces = [(sources[3].at[d], results[3].at[d]) for d in range(4)]
    half = sources[0].shape[0] // 2
    pieces += [(sources[0].at[pl.ds(h * half, half)], results[0].at[pl.ds(h * half, half)]) for h in range(2)]
    pieces += [(sources[i], results[i]) for i in (1, 2, 4)]
    moves = [pltpu.make_async_copy(a, b, sem.at[i]) for i, (a, b) in enumerate(pieces)]
    for move in moves:
        move.start()
    for move in moves:
        move.wait()


def local(grad_partials, master_weights, row_moment, col_moment):
    rows, width = master_weights.shape
    all_rows = rows * lax.axis_size("dp") * lax.axis_size("row")
    full_width = width * lax.axis_size("col")
    half = rows // 2
    rs_n, ag_n = width // CHUNK, rows // AG_ROWS
    early = width - LATE
    message = 2 * LATE + 2 * LANES
    f32 = jnp.float32
    hbm = pl.BlockSpec(memory_space=pltpu.HBM)
    vmem = pl.BlockSpec(memory_space=pltpu.VMEM)
    results = (
        jax.ShapeDtypeStruct((rows, width), f32),
        jax.ShapeDtypeStruct((1, rows), f32),
        jax.ShapeDtypeStruct((1, width), f32),
        jax.ShapeDtypeStruct((4, rows, width), jnp.bfloat16),
        jax.ShapeDtypeStruct((1, 1), f32),
    )
    held = pl.pallas_call(
        functools.partial(kernel, all_rows, full_width),
        out_shape=results,
        in_specs=[hbm, hbm, hbm, hbm],
        out_specs=(vmem,) * 5,
        scratch_shapes=[
            pltpu.VMEM((half, width), f32), pltpu.VMEM((half, width), f32),
            pltpu.VMEM((half, width), f32), pltpu.VMEM((half, width), f32),
            pltpu.VMEM((rows, width), f32), pltpu.VMEM((rows, width), f32),
            pltpu.VMEM((rows, width), f32), pltpu.VMEM((rows, width), f32),
            pltpu.VMEM((1, rows), f32), pltpu.VMEM((1, width), f32),
            pltpu.VMEM((rows, LANES), f32), pltpu.VMEM((rows, LANES), f32),
            pltpu.VMEM((1, width), f32), pltpu.VMEM((8, width), f32),
            pltpu.VMEM((rows, LANES), f32),
            pltpu.VMEM((4, 1, early), f32), pltpu.VMEM((4, 1, early), f32), pltpu.VMEM((4, 1, early), f32),
            pltpu.VMEM((4, 1, rows), f32),
            pltpu.VMEM((16, 1, message), f32), pltpu.VMEM((4, 1, message), f32), pltpu.VMEM((4, 1, LANES), f32),
            pltpu.SemaphoreType.DMA((6,)),
            pltpu.SemaphoreType.DMA((2, 3)), pltpu.SemaphoreType.DMA((2, 2, rs_n)),
            pltpu.SemaphoreType.DMA((7,)), pltpu.SemaphoreType.DMA((7,)),
            pltpu.SemaphoreType.DMA((2, 2)), pltpu.SemaphoreType.DMA((2, ag_n // 2 + 1)),
            pltpu.SemaphoreType.REGULAR((3,)),
        ],
        compiler_params=pltpu.CompilerParams(
            collective_id=0, has_side_effects=True, vmem_limit_bytes=40 * 1024 * 1024),
        cost_estimate=pl.CostEstimate(flops=10 * rows * width, bytes_accessed=40 * rows * width, transcendentals=0),
        name="adafactor",
    )(*[pltpu.with_memory_space_constraint(a, pltpu.HBM) for a in (grad_partials, master_weights, row_moment.reshape(1, rows), col_moment.reshape(1, width))])
    new_master, new_rows, new_cols, copies, rms = pl.pallas_call(
        write_out,
        out_shape=results,
        in_specs=[pl.BlockSpec(memory_space=pl.ANY)] * 5,
        out_specs=(hbm,) * 5,
        scratch_shapes=[pltpu.SemaphoreType.DMA((9,))],
        compiler_params=pltpu.CompilerParams(vmem_limit_bytes=1024 * 1024),
        cost_estimate=pl.CostEstimate(flops=0, bytes_accessed=24 * rows * width, transcendentals=0),
        name="write_out",
    )(*[pltpu.with_memory_space_constraint(a, pltpu.VMEM) for a in held])
    return (new_master, new_rows.reshape(rows), new_cols.reshape(width), copies, rms.reshape(()))


def solution(mesh):
    return jax.shard_map(
        local,
        mesh=mesh,
        in_specs=(P("dp", None, "row", "col"), P(("dp", "row"), "col"), P(("dp", "row")), P("col")),
        out_specs=(P(("dp", "row"), "col"), P(("dp", "row")), P("col"), P(None, "row", "col"), P()),
        check_vma=False,
    )
```

```python
import functools

import jax
import jax.numpy as jnp
from jax import lax
from jax.experimental import pallas as pl
from jax.experimental.pallas import tpu as pltpu
from jax.sharding import PartitionSpec as P

decay_rate = 0.9
step_rate = 0.05
tiny_value = 1e-30

MESH = pl.DeviceIdType.MESH
LANES = 128
CHUNK = 256
LATE = 768
AHEAD = 1
AG_ROWS = 16


def kernel(all_rows, full_width, grads, master, row_mom_hbm, col_mom_hbm,
           new_master, new_rows, new_cols, copies, rms_out,
           opp_l, opp_r, add_r, add_l, own_l, own_r, mine, mast, row_mom, col_mom,
           row_part, w_part, col_part, inv_cols, inv_rows, x_buf, y_buf, d_buf, r_buf, f_buf, g_buf, h_buf,
           load_sem, rs_send, rs_recv, st_send, st_recv, ag_send, ag_recv, ready):
    dp, row, col = lax.axis_index("dp"), lax.axis_index("row"), lax.axis_index("col")
    y, x = row // 4, row % 4
    right, left, far = (dp + 1) % 4, (dp + 3) % 4, (dp + 2) % 4
    rows, width = mine.shape
    half = rows // 2
    strips = rows // 8
    rs_n = width // CHUNK
    early = width - LATE
    early_n = early // CHUNK

    def x_peer(j):
        return {"row": y * 4 + (x + j) % 4}

    def y_peer(j):
        return {"row": ((y + j) % 4) * 4 + x}

    def d_peer(j):
        return {"dp": (dp + j) % 4}

    def c_peer(j):
        return {"col": (col + j) % 4}

    def row_peer(j):
        return {"row": (row + j) % 16}

    def z_peer(j):
        to = (dp * 4 + col + j) % 16
        return {"dp": to // 4, "col": to % 4}

    def signal(sem, peer):
        pl.semaphore_signal(sem, inc=1, device_id=peer, device_id_type=MESH)

    near = [d_peer(1), d_peer(3), x_peer(1), y_peer(1), c_peer(1)]
    back = [x_peer(3), y_peer(3), c_peer(3)]
    barrier = pltpu.get_barrier_semaphore()
    for peer in near:
        signal(barrier, peer)

    loads = [
        pltpu.make_async_copy(grads.at[0, right, pl.ds(0, half)], add_r, load_sem.at[0]),
        pltpu.make_async_copy(grads.at[0, left, pl.ds(half, half)], add_l, load_sem.at[1]),
        pltpu.make_async_copy(grads.at[0, dp], mine, load_sem.at[2]),
        pltpu.make_async_copy(row_mom_hbm, row_mom, load_sem.at[3]),
        pltpu.make_async_copy(col_mom_hbm, col_mom, load_sem.at[4]),
        pltpu.make_async_copy(master, mast, load_sem.at[5]),
    ]
    for load in loads:
        load.start()
    pl.semaphore_wait(barrier, len(near))

    def rs_copy(way, phase, k):
        to = right if way == 0 else left
        at = pl.ds(pl.multiple_of(k * CHUNK, CHUNK), CHUNK)
        low, high = pl.ds(0, half), pl.ds(half, half)
        mid, other = (low, high) if way == 0 else (high, low)
        opp, own, add = (opp_l, own_l, add_r) if way == 0 else (opp_r, own_r, add_l)
        if phase == 0:
            src, dst = grads.at[0, far, mid, at], opp.at[:, at]
        elif phase == 1:
            src, dst = grads.at[0, to, other, at], own.at[other, at]
        else:
            src, dst = add.at[:, at], own.at[mid, at]
        return pltpu.make_async_remote_copy(
            src_ref=src, dst_ref=dst, send_sem=rs_send.at[way, phase], recv_sem=rs_recv.at[way, min(phase, 1), k],
            device_id={"dp": to}, device_id_type=MESH)

    for k in range(AHEAD):
        rs_copy(0, 0, k).start()
        rs_copy(1, 0, k).start()

    for peer in back:
        signal(ready.at[0], peer)
    row_part[...] = jnp.zeros_like(row_part)
    loads[0].wait()
    loads[1].wait()
    loads[2].wait()
    pl.semaphore_wait(ready.at[0], len(back))
    for peer in back:
        signal(ready.at[1], peer)

    def add_strips(add, opp, k):
        at = pl.ds(pl.multiple_of(k * CHUNK, CHUNK), CHUNK)
        for r in range(half // 8):
            down = pl.ds(8 * r, 8)
            add[down, at] = add[down, at] + opp[down, at]

    def take(k):
        at = pl.ds(pl.multiple_of(k * CHUNK, CHUNK), CHUNK)
        for way, own in enumerate((own_l, own_r)):
            pltpu.make_async_copy(own.at[:, at], own.at[:, at], rs_recv.at[way, 1, k]).wait()
        cols = jnp.zeros((8, CHUNK), jnp.float32)
        for r in range(strips):
            down = pl.ds(8 * r, 8)
            g = mine[down, at] + own_l[down, at] + own_r[down, at]
            mine[down, at] = g
            square = g * g
            cols = cols + square
            across = square[:, :LANES]
            for c in range(1, CHUNK // LANES):
                across = across + square[:, c * LANES:(c + 1) * LANES]
            row_part[down] = row_part[down] + across
        col_part[:, at] = jnp.sum(cols, axis=0, keepdims=True)

    def issue(k, more=True):
        if more:
            rs_copy(0, 0, k + AHEAD).start()
            rs_copy(1, 0, k + AHEAD).start()
        rs_copy(0, 1, k).start()
        rs_copy(1, 1, k).start()

    def pass_on(k):
        rs_copy(0, 0, k).wait_recv()
        add_strips(add_r, opp_l, k)
        rs_copy(0, 2, k).start()
        rs_copy(1, 0, k).wait_recv()
        add_strips(add_l, opp_r, k)
        rs_copy(1, 2, k).start()

    @pl.loop(0, early_n + 1)
    def _(k):
        issue(k)

        @pl.when(k >= 2)
        def _():
            take(k - 2)

        pass_on(k)

        @pl.when(k == 4)
        def _():
            pl.semaphore_wait(ready.at[1], len(back))
            for j in (1, 2, 3):
                signal(ready.at[2], y_peer(j))
                signal(ready.at[2], d_peer(j))

        @pl.when(k == 8)
        def _():
            pl.semaphore_wait(ready.at[2], 6)

    def stage_copy(stage, buf, me, peer, j):
        return pltpu.make_async_remote_copy(
            src_ref=buf.at[me], dst_ref=buf.at[me], send_sem=st_send.at[stage],
            recv_sem=st_recv.at[stage], device_id=peer(j), device_id_type=MESH)

    stages = ((x_buf, x, x_peer), (y_buf, y, y_peer), (d_buf, dp, d_peer), (r_buf, col, c_peer),
              (f_buf, row, row_peer), (g_buf, dp, d_peer), (h_buf, col, c_peer))

    def send(stage, value):
        buf, me, peer = stages[stage]
        buf[me] = value
        for j in range(1, buf.shape[0]):
            stage_copy(stage, buf, me, peer, j).start()

    def receive(stage):
        buf = stages[stage][0]
        others = buf.at[pl.ds(1, buf.shape[0] - 1)]
        pltpu.make_async_copy(others, others, st_recv.at[stage]).wait()

    def total_of(buf, slots):
        values = [buf[s] for s in slots]
        while len(values) > 1:
            values = [a + b for a, b in zip(values[::2], values[1::2])]
        return values[0]

    for k in range(early_n + 1, rs_n):
        if k == early_n + 2:
            receive(0)
            send(1, total_of(x_buf, range(4)))
            receive(1)
            send(2, total_of(y_buf, range(4)))
        issue(k, k + AHEAD < rs_n)
        take(k - 2)
        if k == early_n + 1:
            send(0, col_part[:, :early])
        pass_on(k)
    for k in range(rs_n - 2, rs_n):
        take(k)

    eye = lax.broadcasted_iota(jnp.int32, (rows, LANES), 0) == lax.broadcasted_iota(jnp.int32, (rows, LANES), 1)
    row_sums = jnp.sum(row_part[...], axis=1, keepdims=True)
    send(3, jnp.sum(jnp.where(eye, row_sums, 0.0), axis=0, keepdims=True))
    receive(2)
    loads[3].wait()
    loads[4].wait()
    next_early = decay_rate * col_mom[:, :early] + (1.0 - decay_rate) * (total_of(d_buf, range(4)) / all_rows + tiny_value)
    new_cols[:, :early] = next_early
    inv_cols[:, :early] = jnp.broadcast_to(1.0 / next_early, (8, early))

    @pl.loop(0, strips)
    def _(r):
        down = pl.ds(pl.multiple_of(r * 8, 8), 8)
        parts = [jnp.zeros((8, LANES), jnp.float32) for _ in range(4)]
        for c in range(early // LANES):
            lanes = pl.ds(c * LANES, LANES)
            g = mine[down, lanes]
            parts[c % 4] = parts[c % 4] + g * g * inv_cols[:, lanes]
        w_part[down] = (parts[0] + parts[1]) + (parts[2] + parts[3])

    share = (decay_rate * col_mom[:, early:] + (1.0 - decay_rate) * tiny_value) / 64.0
    share = share + col_part[:, early:] * ((1.0 - decay_rate) / all_rows)
    receive(3)
    row_mean = total_of(r_buf, range(4)) / full_width + tiny_value
    next_rows = decay_rate * row_mom[...] + (1.0 - decay_rate) * row_mean
    new_rows[...] = next_rows
    rows_down = jnp.sum(jnp.where(eye, next_rows, 0.0), axis=1, keepdims=True)
    inv_rows[...] = jnp.broadcast_to(1.0 / rows_down, inv_rows.shape)

    weighted = []
    for c in range(early // LANES, width // LANES):
        lanes = pl.ds(c * LANES, LANES)
        parts = [jnp.zeros((8, LANES), jnp.float32) for _ in range(2)]
        for r in range(strips):
            down = pl.ds(8 * r, 8)
            g = mine[down, lanes]
            parts[r % 2] = parts[r % 2] + g * g * inv_rows[down]
        weighted.append(jnp.sum(parts[0] + parts[1], axis=0, keepdims=True))
    parts = [jnp.zeros((8, LANES), jnp.float32) for _ in range(2)]
    for r in range(strips):
        down = pl.ds(8 * r, 8)
        parts[r % 2] = parts[r % 2] + w_part[down] * inv_rows[down]
    rest = jnp.sum(parts[0] + parts[1], axis=0, keepdims=True)
    send(4, jnp.concatenate([share] + weighted + [rest, next_rows], axis=1))
    inv_cols[:, :early] = jnp.broadcast_to(lax.rsqrt(new_cols[:, :early]), (8, early))
    inv_rows[...] = jnp.sqrt(inv_rows[...])
    loads[5].wait()
    receive(4)
    send(5, total_of(f_buf, range(16)))
    receive(5)
    both = total_of(g_buf, range(4))
    next_late = both[:, :LATE]
    ratio = both[:, LATE:2 * LATE] / next_late
    squares = both[:, 2 * LATE:2 * LATE + LANES]
    for c in range(LATE // LANES):
        squares = squares + ratio[:, c * LANES:(c + 1) * LANES]
    send(6, squares)
    scale_mean = jnp.sum(both[:, 2 * LATE + LANES:], axis=(0, 1), keepdims=True) / all_rows
    new_cols[:, early:] = next_late
    inv_cols[:, early:] = jnp.broadcast_to(lax.rsqrt(next_late), (8, LATE))
    receive(6)
    squares = total_of(h_buf, range(4))
    update_sum = jnp.sum(squares, axis=(0, 1), keepdims=True) * scale_mean
    rms_update = jnp.sqrt(update_sum / (float(all_rows) * float(full_width)))
    rms_out[...] = rms_update
    factor = step_rate * jnp.sqrt(scale_mean) / jnp.maximum(1.0, rms_update)
    inv_rows[...] = inv_rows[...] * factor

    ag_n = rows // AG_ROWS
    ag_half = ag_n // 2

    def ag_copy(way, k, passed, early=False):
        to = right if way == 0 else left
        at = pl.ds(pl.multiple_of(k * AG_ROWS, AG_ROWS), AG_ROWS)
        slot = (left if way == 0 else right) if passed else dp
        if early:
            sem = k if way == 0 else k - ag_half
        else:
            sem = ag_half
        return pltpu.make_async_remote_copy(
            src_ref=copies.at[slot, at], dst_ref=copies.at[slot, at], send_sem=ag_send.at[way, int(passed)],
            recv_sem=ag_recv.at[way, sem], device_id={"dp": to}, device_id_type=MESH)

    def give(k):
        base = pl.multiple_of(k * AG_ROWS, AG_ROWS)
        at = pl.ds(base, AG_ROWS)
        scale = inv_rows[at]
        for c in range(width // LANES):
            lanes = pl.ds(c * LANES, LANES)
            across = inv_cols[:, lanes]
            across = jnp.concatenate([across] * (AG_ROWS // 8), axis=0)
            w = mast[at, lanes] - mine[at, lanes] * scale * across
            new_master[at, lanes] = w
            copies[dp, at, lanes] = w.astype(jnp.bfloat16)

    @pl.loop(0, ag_half)
    def _(k):
        give(k)
        ag_copy(0, k, False, True).start()
        give(k + ag_half)
        ag_copy(1, k + ag_half, False, True).start()

    @pl.loop(0, ag_half)
    def _(k):
        ag_copy(0, k, False, True).wait_recv()
        ag_copy(0, k, True).start()
        ag_copy(1, k + ag_half, False, True).wait_recv()
        ag_copy(1, k + ag_half, True).start()
        ag_copy(0, k + ag_half, False).start()
        ag_copy(1, k, False).start()

    for way in (0, 1):
        for phase in (0, 1, 2):
            pltpu.make_async_copy(opp_l, opp_l, rs_send.at[way, phase]).wait()
    for stage, (buf, _, _) in enumerate(stages):
        others = buf.at[pl.ds(1, buf.shape[0] - 1)]
        pltpu.make_async_copy(others, others, st_send.at[stage]).wait()
    for way in (0, 1):
        pltpu.make_async_copy(copies.at[dp], copies.at[dp], ag_send.at[way, 0]).wait()
        passed = copies.at[far, pl.ds(0, half)]
        pltpu.make_async_copy(passed, passed, ag_send.at[way, 1]).wait()
        pltpu.make_async_copy(copies.at[far], copies.at[far], ag_recv.at[way, ag_half]).wait()


def write_out(*refs):
    sources, results, sem = refs[:5], refs[5:10], refs[10]
    pieces = [(sources[3].at[d], results[3].at[d]) for d in range(4)]
    half = sources[0].shape[0] // 2
    pieces += [(sources[0].at[pl.ds(h * half, half)], results[0].at[pl.ds(h * half, half)]) for h in range(2)]
    pieces += [(sources[i], results[i]) for i in (1, 2, 4)]
    moves = [pltpu.make_async_copy(a, b, sem.at[i]) for i, (a, b) in enumerate(pieces)]
    for move in moves:
        move.start()
    for move in moves:
        move.wait()


def local(grad_partials, master_weights, row_moment, col_moment):
    rows, width = master_weights.shape
    all_rows = rows * lax.axis_size("dp") * lax.axis_size("row")
    full_width = width * lax.axis_size("col")
    half = rows // 2
    rs_n, ag_n = width // CHUNK, rows // AG_ROWS
    early = width - LATE
    message = 2 * LATE + 2 * LANES
    f32 = jnp.float32
    hbm = pl.BlockSpec(memory_space=pltpu.HBM)
    vmem = pl.BlockSpec(memory_space=pltpu.VMEM)
    results = (
        jax.ShapeDtypeStruct((rows, width), f32),
        jax.ShapeDtypeStruct((1, rows), f32),
        jax.ShapeDtypeStruct((1, width), f32),
        jax.ShapeDtypeStruct((4, rows, width), jnp.bfloat16),
        jax.ShapeDtypeStruct((1, 1), f32),
    )
    held = pl.pallas_call(
        functools.partial(kernel, all_rows, full_width),
        out_shape=results,
        in_specs=[hbm, hbm, hbm, hbm],
        out_specs=(vmem,) * 5,
        scratch_shapes=[
            pltpu.VMEM((half, width), f32), pltpu.VMEM((half, width), f32),
            pltpu.VMEM((half, width), f32), pltpu.VMEM((half, width), f32),
            pltpu.VMEM((rows, width), f32), pltpu.VMEM((rows, width), f32),
            pltpu.VMEM((rows, width), f32), pltpu.VMEM((rows, width), f32),
            pltpu.VMEM((1, rows), f32), pltpu.VMEM((1, width), f32),
            pltpu.VMEM((rows, LANES), f32), pltpu.VMEM((rows, LANES), f32),
            pltpu.VMEM((1, width), f32), pltpu.VMEM((8, width), f32),
            pltpu.VMEM((rows, LANES), f32),
            pltpu.VMEM((4, 1, early), f32), pltpu.VMEM((4, 1, early), f32), pltpu.VMEM((4, 1, early), f32),
            pltpu.VMEM((4, 1, rows), f32),
            pltpu.VMEM((16, 1, message), f32), pltpu.VMEM((4, 1, message), f32), pltpu.VMEM((4, 1, LANES), f32),
            pltpu.SemaphoreType.DMA((6,)),
            pltpu.SemaphoreType.DMA((2, 3)), pltpu.SemaphoreType.DMA((2, 2, rs_n)),
            pltpu.SemaphoreType.DMA((7,)), pltpu.SemaphoreType.DMA((7,)),
            pltpu.SemaphoreType.DMA((2, 2)), pltpu.SemaphoreType.DMA((2, ag_n // 2 + 1)),
            pltpu.SemaphoreType.REGULAR((3,)),
        ],
        compiler_params=pltpu.CompilerParams(
            collective_id=0, has_side_effects=True, vmem_limit_bytes=40 * 1024 * 1024),
        cost_estimate=pl.CostEstimate(flops=10 * rows * width, bytes_accessed=40 * rows * width, transcendentals=0),
        name="adafactor",
    )(*[pltpu.with_memory_space_constraint(a, pltpu.HBM) for a in (grad_partials, master_weights, row_moment.reshape(1, rows), col_moment.reshape(1, width))])
    new_master, new_rows, new_cols, copies, rms = pl.pallas_call(
        write_out,
        out_shape=results,
        in_specs=[pl.BlockSpec(memory_space=pl.ANY)] * 5,
        out_specs=(hbm,) * 5,
        scratch_shapes=[pltpu.SemaphoreType.DMA((9,))],
        compiler_params=pltpu.CompilerParams(vmem_limit_bytes=1024 * 1024),
        cost_estimate=pl.CostEstimate(flops=0, bytes_accessed=24 * rows * width, transcendentals=0),
        name="write_out",
    )(*[pltpu.with_memory_space_constraint(a, pltpu.VMEM) for a in held])
    return (new_master, new_rows.reshape(rows), new_cols.reshape(width), copies, rms.reshape(()))


def solution(mesh):
    return jax.shard_map(
        local,
        mesh=mesh,
        in_specs=(P("dp", None, "row", "col"), P(("dp", "row"), "col"), P(("dp", "row")), P("col")),
        out_specs=(P(("dp", "row"), "col"), P(("dp", "row")), P("col"), P(None, "row", "col"), P()),
        check_vma=False,
    )
```
